32 devices in a mesh: grp: 2 (over y), seq: 4 (over z), head: 4 (over x, core).
Axes of the slice: x: 2, y: 2, z: 4, core: 2. Of those that a mesh axis runs over, the one named last changes fastest.
Arguments:
- queries: bfloat16 [5120, 8192], P(('grp', 'seq'), 'head'), parts along dimension 0, may hold values from -6 to 6
- keys: bfloat16 [5120, 8192], P(('grp', 'seq'), 'head'), parts along dimension 0, may hold values from -6 to 6
- values: bfloat16 [5120, 8192], P(('grp', 'seq'), 'head'), parts along dimension 0, may hold values from -40 to 40, as said below
- gain: float32 [8192], P('head'), may hold values from 0.5 to 1.5
- head_order: int32 [128], P('grp'), parts along dimension 0, may hold values from 0 to 63, each once
Outputs:
- attended: bfloat16 [5120, 8192], P(('grp', 'seq'), 'head'), parts along dimension 0
- final_state: float32 [128, 128, 128], P(('grp', 'seq'), 'head'), parts along dimension 0
The draws below stay inside these ranges and needn't reach their ends.
There are 2 independent parts, one for each index of `grp`. The reference program is written for one: setup_inputs(seed, part) draws one part's arguments, and reference() takes and returns one part's arrays. A program takes and returns all parts, laid end to end along the dimension named above; an argument that names none is the same for every part. Nothing has to cross between parts.
Inputs may be any that keep to these rules, and one draw needn't show every extreme that they name: `head_order`: each head appears exactly once. values of order one to some tens.
All inputs are finite; a program needn't handle non-finite values.
Results may differ from the reference program's by a relative error of at most 0.005.
Values sent between devices are 32-bit elements; how exact they have to be, the bound alone decides.
No kernel may reach another device: no remote copies, remote signals or barrier semaphores. Data moves between devices by JAX's collectives and lax.ppermute only.
A program may use at most 128 MiB of HBM per device.

```python
import jax
import jax.numpy as jnp
from jax import lax

H = 64
DH = 128
TOK_DEV = 640
TOKENS = 2560
N_SEQ = 4


def draw_values(key, part):
    key_base = jax.random.fold_in(key, 11)
    key_rows = jax.random.fold_in(key, 12)
    key_cols = jax.random.fold_in(key, 13)
    shape = (TOKENS, H * DH)
    base = jnp.clip(jax.random.normal(key_base, shape, jnp.float32), -4.0, 4.0)
    row_scale = jnp.exp(jax.random.uniform(key_rows, (TOKENS, 1), jnp.float32, 0.0, 2.3))
    col_scale = jnp.exp(jax.random.uniform(key_cols, (1, H * DH), jnp.float32, -1.2, 1.2))
    return jnp.clip(base * row_scale * col_scale, -40.0, 40.0).astype(jnp.bfloat16)


def block_levels(key, extent, pieces, low, top_value):
    def one(axis_at, shards_of):
        steps = jax.random.uniform(jax.random.fold_in(jax.random.fold_in(key, 6), axis_at), (shards_of,), jnp.float32, low / len(pieces), top_value / len(pieces))
        return jnp.repeat(jnp.exp(steps), extent[axis_at] // shards_of).reshape((-1,) + (1,) * (len(extent) - axis_at - 1))

    loudness = one(*pieces[0])
    for cut in pieces[1:]:
        loudness = loudness * one(*cut)
    return loudness


def bell_draw(key, shape, scale, most, cuts=(), dtype=jnp.bfloat16):
    values = scale * jax.random.normal(key, shape, jnp.float32)
    if cuts:
        values = values * block_levels(key, shape, cuts, -0.22, 0.18)
    return jnp.clip(values, -most, most).astype(dtype)


def setup_inputs(seed: int = 0, part: int = 0) -> dict:
    streams_of = jax.random.split(jax.random.key(seed), 6)
    part_keys = jax.random.split(jax.random.fold_in(streams_of[5], part), 6)
    return {
        "queries": bell_draw(part_keys[0], (TOKENS, H * DH), 1.0, 6.0, ((0, 4), (1, 4))),
        "keys": bell_draw(part_keys[1], (TOKENS, H * DH), 1.0, 6.0, ((0, 4), (1, 4))),
        "values": draw_values(jax.random.fold_in(jax.random.fold_in(streams_of[5], part), 71), part),
        "gain": jnp.clip(1.0 + 0.1 * jax.random.normal(streams_of[3], (H * DH,), jnp.float32), 0.5, 1.5),
        "head_order": jax.random.permutation(part_keys[4], H).astype(jnp.int32),
    }


def reference(queries, keys, values, gain, head_order):
    q_all = queries.reshape(N_SEQ, TOK_DEV, H, DH)
    k_all = keys.reshape(N_SEQ, TOK_DEV, H, DH)
    v_all = values.reshape(N_SEQ, TOK_DEV, H, DH)
    gain_heads = gain.reshape(H, DH)
    causal = jnp.arange(TOK_DEV)[:, None] >= jnp.arange(TOK_DEV)[None, :]

    def step(carry, block):
        q_blk, k_blk, v_blk = block
        q32 = q_blk.astype(jnp.float32)
        k32 = k_blk.astype(jnp.float32)
        v32 = v_blk.astype(jnp.float32)
        local = jnp.einsum('thd,the->hde', k32, v32)
        prefix_low = carry.astype(jnp.bfloat16).astype(jnp.float32)
        scores = jnp.einsum('thd,uhd->htu', q32, k32)
        scores = jnp.where(causal[None], scores, 0.0).astype(jnp.bfloat16).astype(jnp.float32)
        mixed = jnp.einsum('htu,uhe->the', scores, v32) + jnp.einsum('thd,hde->the', q32, prefix_low)
        meansq = lax.optimization_barrier(jnp.mean(mixed * mixed, axis=-1, keepdims=True))
        normed = mixed / jnp.sqrt(meansq + 1e-06) * gain_heads[None]
        return (carry + local, normed.astype(jnp.bfloat16))
    start = jnp.zeros((H, DH, DH), jnp.float32)
    total_state, outs = lax.scan(step, start, (q_all, k_all, v_all))
    attended = outs.reshape(TOKENS, H * DH)
    final_state = jnp.take(total_state, head_order.astype(jnp.int32), axis=0)
    return (attended, final_state)
```

```python
import jax
import jax.numpy as jnp
from jax import lax
from jax.experimental import pallas as pl
from jax.experimental.pallas import tpu as pltpu
from jax.sharding import PartitionSpec as P

DH = 128
EPS = 1e-06
KEYS_AT_ONCE = 256
BATCHES = (4, 2, 2)


def state_body(k_ref, v_ref, s_ref):
    for i in range(s_ref.shape[0]):
        cols = slice(i * DH, (i + 1) * DH)
        s_ref[i] = lax.dot_general(
            k_ref[:, cols], v_ref[:, cols], (((0,), (0,)), ((), ())),
            preferred_element_type=jnp.float32,
        )


def local_states(keys, values, per):
    rows, width = keys.shape
    heads = width // DH
    return pl.pallas_call(
        state_body,
        grid=(heads // per,),
        in_specs=[pl.BlockSpec((rows, per * DH), lambda i: (0, i))] * 2,
        out_specs=pl.BlockSpec((per, DH, DH), lambda i: (i, 0, 0)),
        out_shape=jax.ShapeDtypeStruct((heads, DH, DH), jnp.float32),
        cost_estimate=pl.CostEstimate(
            flops=2 * rows * width * DH, bytes_accessed=4 * rows * width + 4 * width * DH, transcendentals=0
        ),
        name="local_states",
    )(keys, values)


def causal_body(q_ref, k_ref, v_ref, o_ref):
    rows = q_ref.shape[0]
    for i in range(q_ref.shape[1] // DH):
        cols = slice(i * DH, (i + 1) * DH)
        for at in range(0, rows, KEYS_AT_ONCE):
            size = min(KEYS_AT_ONCE, rows - at)
            here = slice(at, at + size)
            scores = lax.dot_general(
                q_ref[at:, cols], k_ref[here, cols], (((1,), (1,)), ((), ())),
                preferred_element_type=jnp.float32,
            )
            row = lax.broadcasted_iota(jnp.int32, (size, size), 0)
            col = lax.broadcasted_iota(jnp.int32, (size, size), 1)
            top = jnp.where(col <= row, scores[:size], 0.0).astype(jnp.bfloat16)
            part = jnp.dot(top, v_ref[here, cols], preferred_element_type=jnp.float32)
            if at == 0:
                o_ref[here, cols] = part
            else:
                o_ref[here, cols] += part
            if at + size < rows:
                low = scores[size:].astype(jnp.bfloat16)
                part = jnp.dot(low, v_ref[here, cols], preferred_element_type=jnp.float32)
                if at == 0:
                    o_ref[at + size:, cols] = part
                else:
                    o_ref[at + size:, cols] += part


def causal_mix(queries, keys, values, per, first, count):
    rows = queries.shape[0]
    block = pl.BlockSpec((rows, per * DH), lambda i: (0, i + first))
    width = count * per * DH
    return pl.pallas_call(
        causal_body,
        grid=(count,),
        in_specs=[block] * 3,
        out_specs=pl.BlockSpec((rows, per * DH), lambda i: (0, i)),
        out_shape=jax.ShapeDtypeStruct((rows, width), jnp.float32),
        cost_estimate=pl.CostEstimate(
            flops=2 * rows * rows * width, bytes_accessed=10 * rows * width, transcendentals=0
        ),
        name="causal_mix",
    )(queries, keys, values)


def finish_body(q_ref, m_ref, p_ref, g_ref, o_ref):
    for i in range(q_ref.shape[1] // DH):
        cols = slice(i * DH, (i + 1) * DH)
        mixed = m_ref[:, cols] + jnp.dot(
            q_ref[:, cols], p_ref[i], preferred_element_type=jnp.float32
        )
        meansq = jnp.mean(mixed * mixed, axis=-1, keepdims=True)
        o_ref[:, cols] = (mixed * lax.rsqrt(meansq + EPS) * g_ref[:, cols]).astype(o_ref.dtype)


def finish(queries, mixed, prefix_low, gain, per):
    rows, width = queries.shape
    block = pl.BlockSpec((rows, per * DH), lambda i: (0, i))
    return pl.pallas_call(
        finish_body,
        grid=(width // (per * DH),),
        in_specs=[
            block, block,
            pl.BlockSpec((per, DH, DH), lambda i: (i, 0, 0)),
            pl.BlockSpec((1, per * DH), lambda i: (0, i)),
        ],
        out_specs=block,
        out_shape=jax.ShapeDtypeStruct((rows, width), jnp.bfloat16),
        cost_estimate=pl.CostEstimate(
            flops=2 * rows * width * DH, bytes_accessed=8 * rows * width, transcendentals=rows * width // DH
        ),
        name="finish",
    )(queries, mixed, prefix_low, gain.reshape(1, width))


def slots_body(n_src, sizes, local_heads, place_ref, order_ref, *refs):
    out_ref = refs[-1]
    mine = place_ref[0]
    first = place_ref[1] * out_ref.shape[0]
    for j in range(out_ref.shape[0]):
        head = order_ref[first + j]
        source = lax.div(head, local_heads)
        within = lax.rem(head, local_heads)
        apart = lax.bitwise_xor(source, mine)
        slot = jnp.zeros(out_ref.shape[1:], out_ref.dtype)
        at = 0
        for b, size in enumerate(sizes):
            inside = jnp.logical_and(within >= at, within < at + size)
            index = jnp.clip(within - at, 0, size - 1)
            for m in range(n_src):
                wanted = jnp.logical_and(inside, apart == m)
                slot = jnp.where(wanted, refs[b * n_src + m][index], slot)
            at += size
        out_ref[j] = slot


def take_slots(place, order, pieces, n_src, sizes, slots):
    shape = (slots,) + pieces[0].shape[1:]
    return pl.pallas_call(
        lambda *refs: slots_body(n_src, sizes, sum(sizes), *refs),
        in_specs=[pl.BlockSpec(memory_space=pltpu.SMEM)] * 2
        + [pl.BlockSpec(memory_space=pltpu.VMEM)] * len(pieces),
        out_specs=pl.BlockSpec(memory_space=pltpu.VMEM),
        out_shape=jax.ShapeDtypeStruct(shape, jnp.float32),
        name="take_slots",
    )(place, order, *pieces)


def make_on_device(n_seq, n_head):
    pairs_a = [(i, i ^ 1) for i in range(n_seq) if (i ^ 1) < n_seq]
    pairs_b = [(i, ((i - 1) ^ 1) + 1) for i in range(1, n_seq) if ((i - 1) ^ 1) + 1 < n_seq]

    def on_device(queries, keys, values, gain, head_order):
        heads = queries.shape[1] // DH
        per = 2 if heads % 2 == 0 else 1
        n = heads // per
        me = lax.axis_index("seq")
        mine = lax.axis_index("head")
        last = n_seq - 1
        local = local_states(keys, values, per).reshape(n, per, DH, DH)
        even = me % 2 == 0
        out_a = jnp.where(even, 2 * me, 2 * (last - me))
        out_b = jnp.where(even, 2 * (last - me), 2 * me)
        zero = jnp.zeros((per, DH, DH), jnp.float32)
        got_a, got_b = {}, {}
        steps = n + 2 * (n_seq - 2)

        def mine_at(chunk):
            return lax.dynamic_index_in_dim(local, jnp.clip(chunk, 0, n - 1), 0, False)

        for t in range(steps):
            if t < 2:
                send_a = local[t]
            else:
                send_a = mine_at(t - out_a) + got_b.get(t - 2, zero)
            got_a[t] = lax.ppermute(send_a, "seq", pairs_a)
            if 2 <= t < steps - 2:
                send_b = mine_at(t - out_b) + got_a[t - 2]
                got_b[t] = lax.ppermute(send_b, "seq", pairs_b)

        prefix, total = [], []
        for c in range(n):
            before, after = zero, zero
            for s in range(1, n_seq):
                came = (got_a if s % 2 else got_b)[c + 2 * (s - 1)]
                before = jnp.where(me == s, came, before)
            for s in range(n_seq - 1):
                back = (got_b if s % 2 else got_a)[c + 2 * (last - 1 - s)]
                after = jnp.where(me == s, back, after)
            prefix.append(before.astype(jnp.bfloat16))
            total.append(before + local[c] + after)

        sizes, pieces, at = [], [], 0
        for b, count in enumerate(BATCHES):
            count = count * n // sum(BATCHES) if b < len(BATCHES) - 1 else n - at
            batch = jnp.concatenate(total[at:at + count], axis=0)
            at += count
            sizes.append(count * per)
            rows = batch.reshape(count * per, n_head, DH // n_head, DH)
            for m in range(n_head):
                part = lax.dynamic_index_in_dim(rows, lax.bitwise_xor(mine, m), 1, False)
                if m:
                    part = lax.ppermute(part, "head", [(i, i ^ m) for i in range(n_head)])
                pieces.append(part)

        mixed = causal_mix(queries, keys, values, per, 0, n)
        attended = finish(queries, mixed, jnp.concatenate(prefix, axis=0), gain, per)
        place = jnp.stack([mine, me]).astype(jnp.int32)
        final_state = take_slots(
            place, head_order, pieces, n_head, tuple(sizes), head_order.shape[0] // n_seq
        )
        return (attended, final_state)

    return on_device


def solution(mesh):
    return jax.shard_map(
        make_on_device(mesh.shape["seq"], mesh.shape["head"]),
        mesh=mesh,
        in_specs=(
            P(("grp", "seq"), "head"),
            P(("grp", "seq"), "head"),
            P(("grp", "seq"), "head"),
            P("head"),
            P("grp"),
        ),
        out_specs=(P(("grp", "seq"), "head"), P(("grp", "seq"), "head", None)),
        check_vma=False,
    )
```
